128 devices in a mesh: cube: 128 (over x, z, y, core).
Axes of the slice: x: 4, y: 4, z: 4, core: 2. Of those that a mesh axis runs over, the one named last changes fastest.
Arguments:
- gfront: float32 [8192, 2048], P('cube'), as said below
- cfront: float32 [8192, 4096], P('cube'), as said below
- rfront: float32 [8192, 8192], P('cube'), as said below
- gmap: int32 [4, 2048], replicated, may hold values from 0 to 4095, as said below
- cmap: int32 [2, 4096], replicated, may hold values from 0 to 8191, as said below
Outputs:
- gfactor: float32 [8192, 256], P('cube')
- cfactor: float32 [8192, 256], P('cube')
- rfactor: float32 [8192, 512], P('cube')
- rschur: float32 [8192, 8192], P('cube')
The draws below stay inside these ranges and needn't reach their ends.
Inputs may be any that keep to these rules, and one draw needn't show every extreme that they name: Entry i of row q goes to a row of the parent front in block b or block b + 32, where b = i // 64 and blocks have 64 rows; within one row of gmap the entries are distinct and increase along each block. Entry i of row c goes to a row of the root front in block b or block b + 64, where b = i // 64 and blocks have 64 rows; within one row of cmap the entries are distinct and increase along each block. `gfront`: every front is symmetric and positive definite. `cfront`: every front is symmetric and positive definite. `rfront`: the front is symmetric and positive definite.
All inputs are finite; a program needn't handle non-finite values.
Results may differ from the reference program's by a relative error of at most 0.0003.
Values sent between devices are 32-bit elements; how exact they have to be, the bound alone decides.
A program may use at most 128 MiB of HBM per device.

```python
import math
import jax
import jax.numpy as jnp
from jax import lax

TILE = 256
NG = 2048
PG = 1
PC = 1
PR = 2
NC = 4096
NR = 8192
SG = 256
SC = 256
SR = 512
ROWS = 64


def make_fronts(key, count, order):
    key_points = jax.random.fold_in(jax.random.fold_in(key, 7), 0)
    key_sign = jax.random.fold_in(jax.random.fold_in(key, 7), 1)
    key_diag = jax.random.fold_in(jax.random.fold_in(key, 7), 2)
    key_common = jax.random.fold_in(jax.random.fold_in(key, 7), 4)
    points = jax.random.uniform(key_points, (3, count, order), jnp.float32)
    reach = 0.5
    dist = jnp.abs(points[0][:, :, None] - points[0][:, None, :])
    dist = dist + jnp.abs(points[1][:, :, None] - points[1][:, None, :])
    dist = dist + jnp.abs(points[2][:, :, None] - points[2][:, None, :])
    signs = jnp.where(jax.random.bernoulli(key_sign, 0.5, (count, order)), 1.0, -1.0).astype(jnp.float32)
    sign_pair = signs[:, :, None] * signs[:, None, :]
    coupled = jnp.exp(dist * (-1.0 / reach)) * sign_pair
    common = jnp.exp(jax.random.uniform(key_common, (count, order), jnp.float32, math.log(0.5), 0.0))
    coupled = coupled + 0.25 * (common[:, :, None] * common[:, None, :])
    shift = jnp.exp(jax.random.uniform(key_diag, (count, order), jnp.float32, math.log(0.03), math.log(1.5)))
    ids = jnp.arange(order)
    on_diag = (ids[:, None] == ids[None, :])[None, :, :]
    fronts = coupled + jnp.where(on_diag, shift[:, :, None], 0.0)
    return fronts.reshape(count * order, order)


def make_map(key, count, order, rows):
    blocks = order // rows
    keys = jax.random.split(jax.random.fold_in(key, 11), count * blocks)

    def one_block(block_key):
        picked = jax.random.permutation(block_key, 2 * rows - 2)[:rows - 2] + 1
        slots = jnp.concatenate([jnp.zeros((1,), jnp.int32), picked.astype(jnp.int32), jnp.full((1,), 2 * rows - 1, jnp.int32)])
        return jnp.sort(slots)
    slots = jax.vmap(one_block)(keys).reshape(count, blocks, rows)
    block_ids = jnp.arange(blocks, dtype=jnp.int32)[None, :, None]
    mapped = jnp.where(slots < rows, block_ids * rows + slots, (blocks + block_ids) * rows + slots - rows)
    return mapped.reshape(count, order).astype(jnp.int32)


def draw_gfront(key, part):
    return make_fronts(key, 4, NG)


def draw_cfront(key, part):
    return make_fronts(key, 2, NC)


def draw_rfront(key, part):
    return make_fronts(key, 1, NR)


def draw_gmap(key, part):
    return make_map(key, 4, NG, ROWS)


def draw_cmap(key, part):
    return make_map(key, 2, NC, ROWS)


def setup_inputs(seed: int = 0) -> dict:
    seeds = jax.random.split(jax.random.key(seed), 6)
    return {
        "gfront": draw_gfront(jax.random.fold_in(seeds[5], 71), 0),
        "cfront": draw_cfront(jax.random.fold_in(seeds[5], 71), 0),
        "rfront": draw_rfront(jax.random.fold_in(seeds[5], 71), 0),
        "gmap": draw_gmap(jax.random.fold_in(seeds[5], 71), 0),
        "cmap": draw_cmap(jax.random.fold_in(seeds[5], 71), 0),
    }


def partial_factor(front, panels):
    order = front.shape[0]
    ids = jnp.arange(order, dtype=jnp.int32)
    start = order - (panels + 1) * TILE
    pieces = []
    for panel_no in range(panels):
        col_low = start + panel_no * TILE
        col_high = col_low + TILE
        own_cols = front[:, col_low:col_high]
        lower_tri = jnp.linalg.cholesky(front[col_low:col_high, col_low:col_high])
        weights = jax.scipy.linalg.cho_solve((lower_tri, True), own_cols.T).T
        factor = jax.scipy.linalg.solve_triangular(lower_tri, own_cols.T, lower=True).T
        pieces.append(jnp.where(((ids >= col_low) | (ids < start))[:, None], factor, 0.0))
        product = jnp.einsum('rb,nb->rn', weights, own_cols, precision=lax.Precision.HIGHEST)
        remain = (ids >= col_high) | (ids < start)
        trailing = remain[:, None] & remain[None, :]
        front = front - jnp.where(trailing, product, 0.0)
    return (front, jnp.concatenate(pieces, 1))

def kept_ids(order, separator):
    ids = jnp.arange(order, dtype=jnp.int32)
    return (ids < order - separator - TILE) | (ids >= order - TILE)

def place_front(front, separator, front_map):
    order = front.shape[0]
    keep_ids = kept_ids(order, separator)
    keep_mask = keep_ids[:, None] & keep_ids[None, :]
    masked = jnp.where(keep_mask, front, 0.0)
    placed = jnp.zeros((2 * order, 2 * order), front.dtype)
    return placed.at[front_map[:, None], front_map[None, :]].add(masked)

def reference(gfront, cfront, rfront, gmap, cmap):
    g_factors = []
    g_placed = []
    for front_no in range(4):
        block = gfront[front_no * NG:(front_no + 1) * NG]
        done, factor = partial_factor(block, PG)
        g_factors.append(factor)
        g_placed.append(place_front(done, SG, gmap[front_no]))
    c_factors = []
    c_placed = []
    for front_no in range(2):
        block = cfront[front_no * NC:(front_no + 1) * NC] + g_placed[2 * front_no] + g_placed[2 * front_no + 1]
        done, factor = partial_factor(block, PC)
        c_factors.append(factor)
        c_placed.append(place_front(done, SC, cmap[front_no]))
    root = rfront + c_placed[0] + c_placed[1]
    done, rfactor = partial_factor(root, PR)
    rest_ids = kept_ids(NR, SR)
    rest_mask = rest_ids[:, None] & rest_ids[None, :]
    rschur = jnp.where(rest_mask, done, 0.0)
    return (jnp.concatenate(g_factors, 0), jnp.concatenate(c_factors, 0), rfactor, rschur)
```

```python
import jax
import jax.numpy as jnp
from jax import lax
from jax.experimental import pallas as pl
from jax.experimental.pallas import tpu as pltpu
from jax.sharding import PartitionSpec as P

F32 = jnp.float32
BF16 = jnp.bfloat16
HI = lax.Precision.HIGHEST
MESH = pl.DeviceIdType.MESH
NN = ((1,), (0,))
NT = ((1,), (1,))
TILE = 256
MAX_COPIES = 192


def dot32(a, b, dims=NN):
    return lax.dot_general(a, b, (dims, ((), ())), precision=HI, preferred_element_type=F32)


def dot16(a, b, dims=NN):
    return lax.dot_general(a, b, (dims, ((), ())), preferred_element_type=F32)


def split(a):
    high = a.astype(BF16)
    return high, (a - high.astype(F32)).astype(BF16)


def bcast_row(v, j):
    return jnp.broadcast_to(v[j : j + 1, :], (8, 128))


def bcast_lane(v, j):
    return jnp.broadcast_to(v[:, j : j + 1], (8, 128))


def factor_tiles(tiles, tick):
    count = len(tiles)
    sub = lax.broadcasted_iota(jnp.int32, (8, 128), 0)
    tiles = [list(t) for t in tiles]
    outs = [[] for _ in range(count)]
    for r in range(8):
        cols = [[[bcast_lane(t[i], 8 * r + j) for j in range(8)] for i in range(r, 8)] for t in tiles]
        inv = [[None] * 8 for _ in range(count)]
        diag = [jnp.zeros((8, 128), F32) for _ in range(count)]
        for j in range(8):
            for q in range(count):
                b = cols[q]
                p = bcast_row(b[0][j], j)
                t = 1.0 / p
                inv[q][j] = t
                diag[q] = jnp.where(sub == j, p, diag[q])
                for m in range(j + 1, 8):
                    s = bcast_row(b[0][m], j) * t
                    for i in range(8 - r):
                        b[i][m] = b[i][m] - b[i][j] * s
                piv = bcast_row(tiles[q][r], j) * t
                below = jnp.where(sub > j, b[0][j], 0.0)
                tiles[q][r] = tiles[q][r] - below * piv
        for q in range(count):
            v = tiles[q][r]
            for j in range(8):
                piv = bcast_row(v, j) * inv[q][j]
                for i in range(r + 1, 8):
                    tiles[q][i] = tiles[q][i] - cols[q][i - r][j] * piv
            outs[q].append(v * lax.rsqrt(diag[q]))
        tick()
    return outs


def inverse_factor(a_refs, b_refs, t_refs, tick):
    count = len(a_refs)
    eye = lax.broadcasted_iota(jnp.int32, (64, 64), 0) == lax.broadcasted_iota(jnp.int32, (64, 64), 1)
    eye = eye.astype(F32)
    for q in range(count):
        b_refs[q][...] = jnp.zeros((256, 256), F32)
    for k in range(4):
        lo, hi = 64 * k, 64 * k + 64
        tiles = []
        for q in range(count):
            t_refs[q][:, 0:64] = a_refs[q][lo:hi, lo:hi]
            t_refs[q][:, 64:128] = eye
            tiles.append([t_refs[q][8 * i : 8 * i + 8, :] for i in range(8)])
        outs = factor_tiles(tiles, tick)
        for q in range(count):
            for i in range(8):
                t_refs[q][8 * i : 8 * i + 8, :] = outs[q][i]
            g = t_refs[q][:, 64:128]
            if k > 0:
                b_refs[q][lo:hi, 0:lo] = dot32(g, b_refs[q][lo:hi, 0:lo])
            b_refs[q][lo:hi, lo:hi] = g
            if k < 3:
                low = dot32(a_refs[q][hi:, lo:hi], g, NT)
                a_refs[q][hi:, hi:] = a_refs[q][hi:, hi:] - dot32(low, low, NT)
                b_refs[q][hi:, 0:hi] = b_refs[q][hi:, 0:hi] - dot32(low, b_refs[q][lo:hi, 0:hi])
        tick()


def kernel(g_ref, c_ref, r_ref, gm_ref, cm_ref, gf_ref, cf_ref, rf_ref, out_ref,
           pan_g, pan_c, pan_1, pan_0, dia_g, dia_c, dia_0, mat, inv, tile, c_acc,
           ug_send, ug_recv, uc_send, uc_relay, uc_recv, one_send, one_recv,
           send_sems, recv_sems, local_sems):
    me = lax.axis_index("cube")
    core = lax.rem(me, 2)
    y = lax.rem(me // 2, 4)
    z = lax.rem(me // 8, 4)
    x = me // 32
    x2 = lax.rem(x, 2)

    def at(xx, zz, yy):
        return ((lax.rem(xx, 4) * 4 + lax.rem(zz, 4)) * 4 + lax.rem(yy, 4)) * 2 + core

    other_core = me + 1 - 2 * core
    x_pair = me + 32 * (1 - 2 * x2)
    x_far = at(x + 2, z, y)

    used = [0]
    pending = []

    def new_sem(n=1):
        used[0] += n
        assert used[0] <= MAX_COPIES
        return used[0] - n

    def guarded(cond, fn):
        if cond is None:
            fn()
        else:
            pl.when(cond)(fn)

    def send(ref, dst, device, index, recv_index=None, cond=None):
        copy = pltpu.make_async_remote_copy(
            src_ref=ref, dst_ref=dst, send_sem=send_sems.at[index],
            recv_sem=recv_sems.at[index if recv_index is None else recv_index],
            device_id=(device,), device_id_type=MESH)
        guarded(cond, copy.start)
        pending.append((copy, cond))

    def arrived(ref, recv_index, cond=None):
        copy = pltpu.make_async_remote_copy(
            src_ref=ref, dst_ref=ref, send_sem=send_sems.at[0], recv_sem=recv_sems.at[recv_index],
            device_id=(other_core,), device_id_type=MESH)
        guarded(cond, copy.wait_recv)


    def gather_steps(buf, xs):
        xi = {4: x, 2: x2, 1: 0}[xs]

        def block(xx, rows=slice(None)):
            return buf.at[xx, z, y, core, rows]

        def part(half, phase, coord, rows=slice(None), cc=None):
            cc = core if cc is None else cc
            cols = slice(128 * half, 128 * half + 128)
            coord = lax.rem(coord, 4)
            if half == 0:
                if phase == 0:
                    return buf.at[:, coord, y, cc, rows, cols]
                return buf.at[:, :, coord, cc, rows, cols]
            if phase == 0:
                return buf.at[:, z, coord, cc, rows, cols]
            return buf.at[:, coord, :, cc, rows, cols]

        def axis_of(half, phase):
            return "zy"[(half + phase) % 2]

        def ends(half, phase):
            if axis_of(half, phase) == "z":
                return z, at(x, z + 1, y), at(x, z + 3, y)
            return y, at(x, z, y + 1), at(x, z, y + 3)

        top, bottom = slice(0, 32), slice(32, 64)
        sx = new_sem(4)
        if xs == 4:
            send(block(x), block(x), at(x + 1, z, y), sx)
            send(block(x), block(x), at(x + 3, z, y), sx + 1)
            yield
            xm, xp, xo = lax.rem(x + 3, 4), lax.rem(x + 1, 4), lax.rem(x + 2, 4)
            arrived(block(xm), sx)
            send(block(xm, top), block(xm, top), at(x + 1, z, y), sx + 2)
            arrived(block(xp), sx + 1)
            send(block(xp, bottom), block(xp, bottom), at(x + 3, z, y), sx + 3)
            yield
            arrived(block(xo, top), sx + 2)
            arrived(block(xo, bottom), sx + 3)
        elif xs == 2:
            send(block(x2), block(x2), x_pair, sx)
            yield
            arrived(block(1 - x2), sx)
        dd = new_sem(8)
        for phase in range(2):
            s = new_sem(8)
            for h in range(2):
                a, plus, minus = ends(h, phase)
                send(part(h, phase, a), part(h, phase, a), plus, s + 4 * h)
                send(part(h, phase, a), part(h, phase, a), minus, s + 4 * h + 1)
                if phase == 1:
                    send(part(h, 1, a), part(h, 1, a), other_core, dd + 4 * h)
            yield
            for h in range(2):
                a, plus, minus = ends(h, phase)
                arrived(part(h, phase, a + 3), s + 4 * h)
                send(part(h, phase, a + 3, top), part(h, phase, a + 3, top), plus, s + 4 * h + 2)
                arrived(part(h, phase, a + 1), s + 4 * h + 1)
                send(part(h, phase, a + 1, bottom), part(h, phase, a + 1, bottom), minus, s + 4 * h + 3)
                if phase == 1:
                    send(part(h, 1, a + 3), part(h, 1, a + 3), other_core, dd + 4 * h + 1)
                    send(part(h, 1, a + 1), part(h, 1, a + 1), other_core, dd + 4 * h + 2)
            yield
            for h in range(2):
                a, plus, minus = ends(h, phase)
                arrived(part(h, phase, a + 2, top), s + 4 * h + 2)
                arrived(part(h, phase, a + 2, bottom), s + 4 * h + 3)
                if phase == 1:
                    send(part(h, 1, a + 2), part(h, 1, a + 2), other_core, dd + 4 * h + 3)
        yield
        for h in range(2):
            a, plus, minus = ends(h, 1)
            for k, step in enumerate((0, 3, 1, 2)):
                arrived(part(h, 1, a + step, cc=1 - core), dd + 4 * h + k)


    def spread_steps(buf, x_mode, zs, ys):
        yi = jnp.where(y == ys + 1, 1, 0)
        in_y = (y == ys) | (y == ys + 1)
        slot = buf.at[yi, core]
        if x_mode is not None:
            sx = new_sem(3)
            own = in_y & (z == zs)
            if x_mode == "pair":
                send(slot, slot, x_pair, sx, cond=own & (x2 == 1))
                yield
                arrived(slot, sx, own & (x2 == 0))
            else:
                src = own & (x == 3)
                send(slot, slot, at(0, z, y), sx, sx, src)
                send(slot, slot, at(2, z, y), sx + 1, sx, src)
                send(slot, slot, at(1, z, y), sx + 2, sx, src)
                yield
                arrived(slot, sx, own & (x != 3))
        sz = new_sem(3)
        src = in_y & (z == zs)
        for k, step in enumerate((1, 3, 2)):
            send(slot, slot, at(x, zs + step, y), sz + k, sz, src)
        yield
        arrived(slot, sz, in_y & (z != zs))
        sy = new_sem(6)
        for k, step in enumerate((1, 3, 2)):
            send(slot, slot, at(x, z, y + step), sy + 2 + k, sy + yi, in_y)
        yield
        for k in range(2):
            arrived(buf.at[k, core], sy + k, y != ys + k)
        sd = new_sem(1)
        send(buf.at[:, core], buf.at[:, core], other_core, sd)
        yield
        arrived(buf.at[:, 1 - core], sd)

    def finish(gen):
        for _ in gen:
            pass

    def step(*gens):
        for gen in gens:
            next(gen, None)

    in_g = (z == 3) & (y < 2)
    in_c = in_g & (x2 == 1)
    yi01 = jnp.where(y == 1, 1, 0)
    starts = [
        (g_ref.at[:, 1536:1792], pan_g.at[0, z, y, core], None),
        (c_ref.at[:, 3584:3840], pan_c.at[x2, z, y, core], None),
        (r_ref.at[:, 7680:7936], pan_1.at[x, z, y, core], None),
        (g_ref.at[:, 1536:1792], dia_g.at[yi01, core], in_g),
        (c_ref.at[:, 3584:3840], dia_c.at[yi01, core], in_c),
    ]
    copies = [(pltpu.make_async_copy(a, b, local_sems.at[i]), cond) for i, (a, b, cond) in enumerate(starts)]
    for copy, cond in copies:
        guarded(cond, copy.start)

    barrier = pltpu.get_barrier_semaphore()
    peers = [at(x + k, z, y) for k in (1, 2, 3)] + [at(x, z + k, y) for k in (1, 2, 3)]
    peers += [at(x, z, y + k) for k in (1, 2, 3)] + [other_core]
    for peer in peers:
        pl.semaphore_signal(barrier, inc=1, device_id=(peer,), device_id_type=MESH)
    c_acc[...] = c_ref[...]
    for copy, cond in copies:
        guarded(cond, copy.wait)
    pl.semaphore_wait(barrier, len(peers))

    spread_g = spread_steps(dia_g, None, 3, 0)
    spread_c = spread_steps(dia_c, "pair", 3, 0)
    gather_g = gather_steps(pan_g, 1)
    gather_c = gather_steps(pan_c, 2)
    gather_1 = gather_steps(pan_1, 4)
    step(spread_c, spread_g, gather_c, gather_g, gather_1)
    step(spread_c, spread_g, gather_c, gather_g, gather_1)
    step(spread_c, spread_g)
    step(spread_c, spread_g)
    finish(spread_g)
    finish(spread_c)

    queue = [gather_g, gather_c, gather_1, gather_g, gather_c, gather_1, gather_g, gather_c, gather_g, gather_c,
             gather_1, gather_g, gather_c, gather_1]
    ticks = [0]

    def pump(every):
        def tick():
            ticks[0] += 1
            if ticks[0] % every == 0 and queue:
                step(queue.pop(0))
        return tick

    mat[0] = dia_g[...].reshape(256, 256)
    mat[1] = dia_c[...].reshape(256, 256)
    inverse_factor([mat.at[0], mat.at[1]], [inv.at[0], inv.at[1]], [tile.at[0], tile.at[1]], pump(2))

    low_g = dot32(g_ref[:, 1536:1792], inv[0], NT)
    gf_ref[...] = low_g
    wg_hi, wg_lo = split(dot32(low_g, inv[0]))
    wg_both = jnp.concatenate([wg_hi, wg_lo], 0)
    low_c = dot32(c_ref[:, 3584:3840], inv[1], NT)
    cf_ref[...] = low_c
    wc_hi, wc_lo = split(dot32(low_c, inv[1]))
    wc_both = jnp.concatenate([wc_hi, wc_lo], 0)

    def times_panel(both, high, panel):
        p_hi, p_lo = split(panel)
        prod = dot16(both, p_hi, NT)
        return prod[:64] + prod[64:] + dot16(high, p_lo, NT)

    def rows_of(buf, n):
        xx = n // 8
        zz = lax.rem(n // 2, 4) if not isinstance(n, int) else n // 2 % 4
        yy = 2 * (n % 2) if isinstance(n, int) else pl.multiple_of(2 * lax.rem(n, 2), 2)
        return buf[xx, zz, pl.ds(yy, 2)].reshape(256, 256)

    def lanes(n):
        return pl.ds(n * 256 if isinstance(n, int) else pl.multiple_of(n * 256, 256), 256)

    def map_row(map_ref, front, where):
        rows = map_ref[:, where]
        row = rows[0:1]
        for k in range(1, rows.shape[0]):
            row = jnp.where(front == k, rows[k : k + 1], row)
        return row

    def row_pick(map_ref, front, blk, base, keep):
        pair = map_row(map_ref, front, pl.ds(pl.multiple_of(128 * (blk // 2), 128), 128))
        mine = jnp.where(lax.rem(blk, 2) == 0, pair[:, 0:64], pair[:, 64:128])
        want = base + lax.broadcasted_iota(jnp.int32, (64, 64), 0)
        return jnp.where((mine == want) & keep, 1.0, 0.0).astype(BF16)

    def picked(pick, block):
        hi, lo = split(block)
        both = dot16(pick, jnp.concatenate([hi, lo], 1)).astype(BF16)
        return jnp.concatenate([both[:, 0:256], both[:, 256:512]], 0)

    def expand(map_ref, fronts, picks, blocks, n, base):
        lhs = jnp.concatenate([picked(p, b) for p, b in zip(picks, blocks)], 1)
        maps = [map_row(map_ref, f, lanes(n)) for f in fronts]
        where_to = jnp.concatenate(maps, 1)
        out = []
        for start in (0, base):
            want = 256 * n + start + lax.broadcasted_iota(jnp.int32, (256, 512), 0)
            hot = jnp.where(where_to == want, 1.0, 0.0).astype(BF16)
            prod = dot16(lhs, hot, NT)
            out.append(prod[:64] + prod[64:])
        return out

    def g_rows(n):
        return g_ref[:, lanes(n)] - times_panel(wg_both, wg_hi, rows_of(pan_g, n))

    finish(gather_g)
    one_send[0] = g_rows(5)
    s_one = new_sem(1)
    send(one_send.at[0], one_recv.at[0], x_pair, s_one)
    g_slots = (0, 1, 2, 3, 4, 7)
    for i, n in enumerate(g_slots):
        ug_send[i] = g_rows(n)
    s_g = new_sem(1)
    send(ug_send, ug_recv, x_pair, s_g)
    blk_g = lax.rem(me, 32)
    keep_g = (blk_g < 24) | (blk_g >= 28)
    base_g = 64 * lax.rem(me, 64)
    fronts_g = (x, x + 1 - 2 * x2)
    picks_g = [row_pick(gm_ref, f, blk_g, base_g, keep_g) for f in fronts_g]

    def add_g(n, own, other):
        lo, hi = expand(gm_ref, fronts_g, picks_g, [own, other], n, 2048)
        c_acc[:, lanes(n)] += lo
        c_acc[:, lanes(n + 8)] += hi

    arrived(one_recv.at[0], s_one)
    add_g(5, one_send[0], one_recv[0])

    def c_rows(n):
        return c_acc[:, lanes(n)] - times_panel(wc_both, wc_hi, rows_of(pan_c, n))

    finish(gather_c)
    one_send[1] = c_rows(13)
    s_one = new_sem(1)
    send(one_send.at[1], one_recv.at[1], x_far, s_one)
    while queue:
        step(queue.pop(0))
    blk_c = lax.rem(me, 64)
    keep_c = (blk_c < 56) | (blk_c >= 60)
    fronts_c = (x // 2, 1 - x // 2)
    picks_c = [row_pick(cm_ref, f, blk_c, 64 * me, keep_c) for f in fronts_c]

    arrived(one_recv.at[1], s_one)
    lo, hi = expand(cm_ref, fronts_c, picks_c, [one_send[1], one_recv[1]], 13, 4096)
    out_ref[:, 3328:3584] = r_ref[:, 3328:3584] + lo
    own_0 = r_ref[:, 7424:7680] + hi
    pan_0[x, z, y, core] = own_0
    in_0 = (x == 3) & (z == 2) & (y >= 2)

    @pl.when(in_0)
    def _():
        dia_0[jnp.where(y == 3, 1, 0), core] = own_0

    spread_0 = spread_steps(dia_0, "root", 2, 2)
    gather_0 = gather_steps(pan_0, 4)
    step(spread_0, gather_0)
    arrived(ug_recv, s_g)
    for i, n in enumerate(g_slots):
        add_g(n, ug_send[i], ug_recv[i])
        if i % 2 == 1:
            step(spread_0)

    def c_group(s):
        return jnp.where(s == 13, 15, s)

    def fill(s, _):
        uc_send[s] = c_rows(c_group(s))
        return 0

    s_c = new_sem(4)
    first, second = pl.ds(0, 7), pl.ds(7, 7)
    lax.fori_loop(0, 7, fill, 0)
    send(uc_send.at[first], uc_relay.at[first], at(x + 1, z, y), s_c)
    lax.fori_loop(7, 14, fill, 0)
    send(uc_send.at[second], uc_relay.at[second], at(x + 3, z, y), s_c + 1)
    finish(spread_0)

    def relay():
        arrived(uc_relay.at[first], s_c)
        send(uc_relay.at[first], uc_recv.at[first], at(x + 1, z, y), s_c + 2)
        yield
        arrived(uc_relay.at[second], s_c + 1)
        send(uc_relay.at[second], uc_recv.at[second], at(x + 3, z, y), s_c + 3)
        yield

    relay_c = relay()
    queue = [gather_0, gather_0, gather_0, relay_c, gather_0, relay_c, gather_0, gather_1, gather_1]

    def pump0(every):
        def tick():
            ticks[0] += 1
            if ticks[0] % every == 0 and queue:
                step(queue.pop(0))
        return tick

    mat[0] = dia_0[...].reshape(256, 256)
    inverse_factor([mat.at[0]], [inv.at[0]], [tile.at[0]], pump0(4))
    finish(gather_1)
    inv_0 = inv[0]
    cross = pan_1[3, 2, 2:4].reshape(256, 256)
    low_x = dot32(inv_0, cross)
    mat[1] = pan_1[3, 3, 0:2].reshape(256, 256) - dot32(low_x, low_x, ((0,), (0,)))
    inverse_factor([mat.at[1]], [inv.at[1]], [tile.at[1]], pump0(2))
    inv_1 = inv[1]

    low_0 = dot32(own_0, inv_0, NT)
    rf_ref[:, 0:256] = low_0
    own_1 = r_ref[:, 7680:7936] - dot32(low_0, low_x)
    low_1 = dot32(own_1, inv_1, NT)
    rf_ref[:, 256:512] = jnp.where(in_0, 0.0, low_1)
    w_1 = dot32(low_1, inv_1)
    m_0 = dot32(low_0 - dot32(w_1, low_x, NT), inv_0)
    w_hi, w_lo = split(jnp.concatenate([m_0, w_1], 1))
    w_both = jnp.concatenate([w_hi, w_lo], 0)

    while queue:
        step(queue.pop(0))
    finish(relay_c)
    arrived(uc_recv.at[first], s_c + 2)
    arrived(uc_recv.at[second], s_c + 3)

    def add_c(s, _):
        n = c_group(s)
        lo, hi = expand(cm_ref, fronts_c, picks_c, [uc_send[s], uc_recv[s]], n, 4096)
        out_ref[:, lanes(n)] = r_ref[:, lanes(n)] + lo
        out_ref[:, lanes(n + 16)] = r_ref[:, lanes(n + 16)] + hi
        return 0

    lax.fori_loop(0, 14, add_c, 0)
    out_ref[:, 3584:3840] = r_ref[:, 3584:3840]
    finish(gather_0)

    row_kept = jnp.logical_not((x == 3) & (((z == 2) & (y >= 2)) | ((z == 3) & (y < 2))))

    def last(t, _):
        n = jnp.where(t >= 29, t + 2, t)
        panel = jnp.concatenate([rows_of(pan_0, n), rows_of(pan_1, n)], 1)
        res = out_ref[:, lanes(n)] - times_panel(w_both, w_hi, panel)
        out_ref[:, lanes(n)] = jnp.where(row_kept, res, 0.0)
        return 0

    lax.fori_loop(0, 30, last, 0)
    out_ref[:, 7424:7936] = jnp.zeros((64, 512), F32)

    for copy, cond in pending:
        guarded(cond, copy.wait_send)


def local(gfront, cfront, rfront, gmap, cmap):
    vmem = pl.BlockSpec(memory_space=pltpu.VMEM)
    block = (64, 256)
    return pl.pallas_call(
        kernel,
        out_shape=(
            jax.ShapeDtypeStruct((64, 256), F32),
            jax.ShapeDtypeStruct((64, 256), F32),
            jax.ShapeDtypeStruct((64, 512), F32),
            jax.ShapeDtypeStruct((64, 8192), F32),
        ),
        in_specs=[vmem] * 5,
        out_specs=(vmem,) * 4,
        scratch_shapes=[
            pltpu.VMEM((1, 4, 4, 2) + block, F32),
            pltpu.VMEM((2, 4, 4, 2) + block, F32),
            pltpu.VMEM((4, 4, 4, 2) + block, F32),
            pltpu.VMEM((4, 4, 4, 2) + block, F32),
            pltpu.VMEM((2, 2) + block, F32),
            pltpu.VMEM((2, 2) + block, F32),
            pltpu.VMEM((2, 2) + block, F32),
            pltpu.VMEM((2, 256, 256), F32),
            pltpu.VMEM((2, 256, 256), F32),
            pltpu.VMEM((2, 64, 128), F32),
            pltpu.VMEM((64, 4096), F32),
            pltpu.VMEM((6,) + block, F32),
            pltpu.VMEM((6,) + block, F32),
            pltpu.VMEM((14,) + block, F32),
            pltpu.VMEM((14,) + block, F32),
            pltpu.VMEM((14,) + block, F32),
            pltpu.VMEM((2,) + block, F32),
            pltpu.VMEM((2,) + block, F32),
            pltpu.SemaphoreType.DMA((MAX_COPIES,)),
            pltpu.SemaphoreType.DMA((MAX_COPIES,)),
            pltpu.SemaphoreType.DMA((8,)),
        ],
        compiler_params=pltpu.CompilerParams(
            collective_id=0, has_side_effects=True, vmem_limit_bytes=60 * 1024 * 1024
        ),
    )(gfront, cfront, rfront, gmap, cmap)


def solution(mesh):
    rows = P("cube", None)
    return jax.shard_map(
        local,
        mesh=mesh,
        in_specs=(rows, rows, rows, P(), P()),
        out_specs=(rows, rows, rows, rows),
        check_vma=False,
    )
```

```python
import jax
import jax.numpy as jnp
from jax import lax
from jax.experimental import pallas as pl
from jax.experimental.pallas import tpu as pltpu
from jax.sharding import PartitionSpec as P

F32 = jnp.float32
BF16 = jnp.bfloat16
HI = lax.Precision.HIGHEST
MESH = pl.DeviceIdType.MESH
NN = ((1,), (0,))
NT = ((1,), (1,))
TILE = 256
MAX_COPIES = 224


def dot32(a, b, dims=NN):
    return lax.dot_general(a, b, (dims, ((), ())), precision=HI, preferred_element_type=F32)


def dot16(a, b, dims=NN):
    return lax.dot_general(a, b, (dims, ((), ())), preferred_element_type=F32)


def split(a):
    high = a.astype(BF16)
    return high, (a - high.astype(F32)).astype(BF16)


def bcast_row(v, j):
    return jnp.broadcast_to(v[j : j + 1, :], (8, 128))


def bcast_lane(v, j):
    return jnp.broadcast_to(v[:, j : j + 1], (8, 128))


def factor_tiles(tiles, tick):
    count = len(tiles)
    sub = lax.broadcasted_iota(jnp.int32, (8, 128), 0)
    tiles = [list(t) for t in tiles]
    outs = [[] for _ in range(count)]
    for r in range(8):
        cols = [[[bcast_lane(t[i], 8 * r + j) for j in range(8)] for i in range(r, 8)] for t in tiles]
        inv = [[None] * 8 for _ in range(count)]
        diag = [jnp.zeros((8, 128), F32) for _ in range(count)]
        for j in range(8):
            for q in range(count):
                b = cols[q]
                p = bcast_row(b[0][j], j)
                t = 1.0 / p
                inv[q][j] = t
                diag[q] = jnp.where(sub == j, p, diag[q])
                for m in range(j + 1, 8):
                    s = bcast_row(b[0][m], j) * t
                    for i in range(8 - r):
                        b[i][m] = b[i][m] - b[i][j] * s
                piv = bcast_row(tiles[q][r], j) * t
                below = jnp.where(sub > j, b[0][j], 0.0)
                tiles[q][r] = tiles[q][r] - below * piv
        for q in range(count):
            v = tiles[q][r]
            for j in range(8):
                piv = bcast_row(v, j) * inv[q][j]
                for i in range(r + 1, 8):
                    tiles[q][i] = tiles[q][i] - cols[q][i - r][j] * piv
            outs[q].append(v * lax.rsqrt(diag[q]))
        tick()
    return outs


def inverse_factor(a_refs, b_refs, t_refs, tick, extra=None):
    count = len(a_refs)
    eye = lax.broadcasted_iota(jnp.int32, (64, 64), 0) == lax.broadcasted_iota(jnp.int32, (64, 64), 1)
    eye = eye.astype(F32)
    later = []

    def both_ticks():
        for _ in range(count):
            if later:
                later.pop(0)()
        tick()

    for q in range(count):
        b_refs[q][...] = jnp.zeros((256, 256), F32)
    for k in range(4):
        lo, hi = 64 * k, 64 * k + 64
        tiles = []
        for q in range(count):
            t_refs[q][:, 0:64] = a_refs[q][lo:hi, lo:hi]
            t_refs[q][:, 64:128] = eye
            tiles.append([t_refs[q][8 * i : 8 * i + 8, :] for i in range(8)])
        outs = factor_tiles(tiles, both_ticks)
        while later:
            later.pop(0)()
        waiting = []
        for q in range(count):
            for i in range(8):
                t_refs[q][8 * i : 8 * i + 8, :] = outs[q][i]
            waiting.append(rest_of_block(a_refs[q], b_refs[q], t_refs[q][:, 64:128], lo, hi))
        later = [fn for group in zip(*waiting) for fn in group]
        if extra is not None:
            later += extra(k)
    while later:
        later.pop(0)()


def rest_of_block(a, b, g, lo, hi):
    end = hi + 64
    if lo < 192:
        low = dot32(a[hi:end, lo:hi], g, NT)
        a[hi:end, hi:end] = a[hi:end, hi:end] - dot32(low, low, NT)
    rest = []
    keep = {}

    def rest_low():
        keep["low"] = dot32(a[end:, lo:hi], g, NT)
        a[end:, hi:end] = a[end:, hi:end] - dot32(keep["low"], low, NT)

    def rest_square():
        a[end:, end:] = a[end:, end:] - dot32(keep["low"], keep["low"], NT)

    def own_inverse():
        if lo > 0:
            b[lo:hi, 0:lo] = dot32(g, b[lo:hi, 0:lo])
        b[lo:hi, lo:hi] = g

    def next_inverse():
        b[hi:end, 0:hi] = b[hi:end, 0:hi] - dot32(low, b[lo:hi, 0:hi])

    def rest_inverse():
        b[end:, 0:hi] = b[end:, 0:hi] - dot32(keep["low"], b[lo:hi, 0:hi])

    if lo < 128:
        rest += [rest_low, rest_square]
    rest.append(own_inverse)
    if lo < 192:
        rest.append(next_inverse)
    if lo < 128:
        rest.append(rest_inverse)
    return rest


def kernel(g_hbm, c_hbm, r_hbm, gm_hbm, cm_hbm, gf_ref, cf_ref, rf_ref, out_hbm,
           g_ref, out_ref, gm_ref, cm_ref, pan_g, pan_c, pan_1, pan_0, dia_g, dia_c, dia_0, mat, inv, tile, c_acc,
           ug_send, ug_recv, uc_send, uc_relay, uc_recv, one_send, one_recv,
           low_x, x_mat, own_1, m_own, send_sems, recv_sems, local_sems, out_sems):
    me = lax.axis_index("cube")
    core = lax.rem(me, 2)
    y = lax.rem(me // 2, 4)
    z = lax.rem(me // 8, 4)
    x = me // 32
    x2 = lax.rem(x, 2)

    def at(xx, zz, yy):
        return ((lax.rem(xx, 4) * 4 + lax.rem(zz, 4)) * 4 + lax.rem(yy, 4)) * 2 + core

    other_core = me + 1 - 2 * core
    x_pair = me + 32 * (1 - 2 * x2)
    x_far = at(x + 2, z, y)

    used = [0]
    pending = []

    def new_sem(n=1):
        used[0] += n
        assert used[0] <= MAX_COPIES
        return used[0] - n

    def guarded(cond, fn):
        if cond is None:
            fn()
        else:
            pl.when(cond)(fn)

    def send(ref, dst, device, index, recv_index=None, cond=None):
        copy = pltpu.make_async_remote_copy(
            src_ref=ref, dst_ref=dst, send_sem=send_sems.at[index],
            recv_sem=recv_sems.at[index if recv_index is None else recv_index],
            device_id=(device,), device_id_type=MESH)
        guarded(cond, copy.start)
        pending.append((copy, cond))

    def arrived(ref, recv_index, cond=None):
        copy = pltpu.make_async_remote_copy(
            src_ref=ref, dst_ref=ref, send_sem=send_sems.at[0], recv_sem=recv_sems.at[recv_index],
            device_id=(other_core,), device_id_type=MESH)
        guarded(cond, copy.wait_recv)


    def gather_steps(buf, xs):
        xi = {4: x, 2: x2, 1: 0}[xs]

        def block(xx, rows=slice(None)):
            return buf.at[xx, z, y, core, rows]

        def part(half, phase, coord, rows=slice(None), cc=None):
            cc = core if cc is None else cc
            cols = slice(128 * half, 128 * half + 128)
            coord = lax.rem(coord, 4)
            if half == 0:
                if phase == 0:
                    return buf.at[:, coord, y, cc, rows, cols]
                return buf.at[:, :, coord, cc, rows, cols]
            if phase == 0:
                return buf.at[:, z, coord, cc, rows, cols]
            return buf.at[:, coord, :, cc, rows, cols]

        def axis_of(half, phase):
            return "zy"[(half + phase) % 2]

        def ends(half, phase):
            if axis_of(half, phase) == "z":
                return z, at(x, z + 1, y), at(x, z + 3, y)
            return y, at(x, z, y + 1), at(x, z, y + 3)

        top, bottom = slice(0, 32), slice(32, 64)
        sx = new_sem(4)
        if xs == 4:
            send(block(x), block(x), at(x + 1, z, y), sx)
            send(block(x), block(x), at(x + 3, z, y), sx + 1)
            yield
            xm, xp, xo = lax.rem(x + 3, 4), lax.rem(x + 1, 4), lax.rem(x + 2, 4)
            arrived(block(xm), sx)
            send(block(xm, top), block(xm, top), at(x + 1, z, y), sx + 2)
            arrived(block(xp), sx + 1)
            send(block(xp, bottom), block(xp, bottom), at(x + 3, z, y), sx + 3)
            yield
            arrived(block(xo, top), sx + 2)
            arrived(block(xo, bottom), sx + 3)
        elif xs == 2:
            send(block(x2), block(x2), x_pair, sx)
            yield
            arrived(block(1 - x2), sx)
        dd = new_sem(8)
        for phase in range(2):
            s = new_sem(8)
            for h in range(2):
                a, plus, minus = ends(h, phase)
                send(part(h, phase, a), part(h, phase, a), plus, s + 4 * h)
                send(part(h, phase, a), part(h, phase, a), minus, s + 4 * h + 1)
                if phase == 1:
                    send(part(h, 1, a), part(h, 1, a), other_core, dd + 4 * h)
            yield
            for h in range(2):
                a, plus, minus = ends(h, phase)
                arrived(part(h, phase, a + 3), s + 4 * h)
                send(part(h, phase, a + 3, top), part(h, phase, a + 3, top), plus, s + 4 * h + 2)
                arrived(part(h, phase, a + 1), s + 4 * h + 1)
                send(part(h, phase, a + 1, bottom), part(h, phase, a + 1, bottom), minus, s + 4 * h + 3)
                if phase == 1:
                    send(part(h, 1, a + 3), part(h, 1, a + 3), other_core, dd + 4 * h + 1)
                    send(part(h, 1, a + 1), part(h, 1, a + 1), other_core, dd + 4 * h + 2)
            yield
            for h in range(2):
                a, plus, minus = ends(h, phase)
                arrived(part(h, phase, a + 2, top), s + 4 * h + 2)
                arrived(part(h, phase, a + 2, bottom), s + 4 * h + 3)
                if phase == 1:
                    send(part(h, 1, a + 2), part(h, 1, a + 2), other_core, dd + 4 * h + 3)
        yield
        for h in range(2):
            a, plus, minus = ends(h, 1)
            for k, step in enumerate((0, 3, 1, 2)):
                arrived(part(h, 1, a + step, cc=1 - core), dd + 4 * h + k)


    def spread_steps(buf, x_mode, zs, ys):
        yi = jnp.where(y == ys + 1, 1, 0)
        in_y = (y == ys) | (y == ys + 1)
        slot = buf.at[yi, core]
        if x_mode is not None:
            sx = new_sem(3)
            own = in_y & (z == zs)
            if x_mode == "pair":
                send(slot, slot, x_pair, sx, cond=own & (x2 == 1))
                yield
                arrived(slot, sx, own & (x2 == 0))
            else:
                src = own & (x == 3)
                send(slot, slot, at(0, z, y), sx, sx, src)
                send(slot, slot, at(2, z, y), sx + 1, sx, src)
                send(slot, slot, at(1, z, y), sx + 2, sx, src)
                yield
                arrived(slot, sx, own & (x != 3))
        left, right = (slice(None), slice(0, 128)), (slice(None), slice(128, 256))
        s1 = new_sem(8)
        src = in_y & (z == zs)
        zline = z == zs
        one = buf.at[(yi, core) + left]
        two = buf.at[(yi, core) + right]
        for k, inc in enumerate((1, 3, 2)):
            send(one, one, at(x, zs + inc, y), s1 + k, s1, src)
            send(two, two, at(x, zs, y + inc), s1 + 3 + k, s1 + 3 + yi, src)
        yield
        arrived(one, s1, in_y & (z != zs))
        for k in range(2):
            arrived(buf.at[(k, core) + right], s1 + 3 + k, zline & (y != ys + k))
        s2 = new_sem(8)
        pair = buf.at[(slice(None), core) + right]
        for k, inc in enumerate((1, 3, 2)):
            send(one, one, at(x, z, y + inc), s2 + k, s2 + yi, in_y)
            send(pair, pair, at(x, zs + inc, y), s2 + 3 + k, s2 + 3, zline)
        yield
        for k in range(2):
            arrived(buf.at[(k, core) + left], s2 + k, y != ys + k)
        arrived(pair, s2 + 3, z != zs)
        sd = new_sem(1)
        send(buf.at[:, core], buf.at[:, core], other_core, sd)
        yield
        arrived(buf.at[:, 1 - core], sd)

    def finish(gen):
        for _ in gen:
            pass

    def step(*gens):
        for gen in gens:
            next(gen, None)

    in_g = (z == 3) & (y < 2)
    in_c = in_g & (x2 == 1)
    yi01 = jnp.where(y == 1, 1, 0)
    starts = [
        (g_hbm.at[:, 1536:1792], pan_g.at[0, z, y, core], None),
        (c_hbm.at[:, 3584:3840], pan_c.at[x2, z, y, core], None),
        (g_hbm.at[:, 1536:1792], dia_g.at[yi01, core], in_g),
        (c_hbm.at[:, 3584:3840], dia_c.at[yi01, core], in_c),
        (r_hbm.at[:, 7680:7936], pan_1.at[x, z, y, core], None),
        (g_hbm, g_ref, None),
        (gm_hbm, gm_ref, None),
        (cm_hbm, cm_ref, None),
        (c_hbm, c_acc, None),
        (r_hbm, out_ref, None),
    ]
    loads = [(pltpu.make_async_copy(a, b, local_sems.at[i]), cond) for i, (a, b, cond) in enumerate(starts)]
    for copy, cond in loads:
        guarded(cond, copy.start)

    barrier = pltpu.get_barrier_semaphore()
    peers = [at(x + k, z, y) for k in (1, 2, 3)] + [at(x, z + k, y) for k in (1, 2, 3)]
    peers += [at(x, z, y + k) for k in (1, 2, 3)] + [other_core]
    for peer in peers:
        pl.semaphore_signal(barrier, inc=1, device_id=(peer,), device_id_type=MESH)
    for copy, cond in loads[:4]:
        guarded(cond, copy.wait)
    pl.semaphore_wait(barrier, len(peers))

    spread_g = spread_steps(dia_g, None, 3, 0)
    spread_c = spread_steps(dia_c, "pair", 3, 0)
    gather_g = gather_steps(pan_g, 1)
    gather_c = gather_steps(pan_c, 2)
    gather_1 = gather_steps(pan_1, 4)
    step(spread_c, spread_g, gather_c, gather_g)
    step(spread_c, gather_c)
    step(spread_g, gather_g)
    step(spread_c, gather_c)
    step(spread_g, spread_c, gather_g, gather_c)
    finish(spread_g)
    finish(spread_c)

    def timed(plan):
        count = [0]

        def tick():
            count[0] += 1
            for fn in plan.get(count[0], ()):
                if callable(fn):
                    fn()
                else:
                    step(fn)
        return tick

    for copy, cond in loads[4:]:
        copy.wait()
    mat[0] = dia_g[...].reshape(256, 256)
    mat[1] = dia_c[...].reshape(256, 256)
    inverse_factor([mat.at[0], mat.at[1]], [inv.at[0], inv.at[1]], [tile.at[0], tile.at[1]], timed({
        2: [gather_1], 7: [gather_1], 10: [gather_g], 12: [gather_1], 15: [gather_c], 17: [gather_1],
        20: [gather_g], 23: [gather_1], 28: [gather_c]}))

    low_g = dot32(pan_g[0, z, y, core], inv[0], NT)
    gf_ref[...] = low_g
    wg_hi, wg_lo = split(dot32(low_g, inv[0]))
    wg_both = jnp.concatenate([wg_hi, wg_lo], 0)
    low_c = dot32(pan_c[x2, z, y, core], inv[1], NT)
    cf_ref[...] = low_c
    wc_hi, wc_lo = split(dot32(low_c, inv[1]))
    wc_both = jnp.concatenate([wc_hi, wc_lo], 0)

    def times_panel(both, high, panel):
        p_hi, p_lo = split(panel)
        prod = dot16(both, p_hi, NT)
        return prod[:64] + prod[64:] + dot16(high, p_lo, NT)

    def rows_of(buf, n):
        xx = n // 8
        zz = lax.rem(n // 2, 4) if not isinstance(n, int) else n // 2 % 4
        yy = 2 * (n % 2) if isinstance(n, int) else pl.multiple_of(2 * lax.rem(n, 2), 2)
        return buf[xx, zz, pl.ds(yy, 2)].reshape(256, 256)

    def lanes(n):
        return pl.ds(n * 256 if isinstance(n, int) else pl.multiple_of(n * 256, 256), 256)

    def map_row(map_ref, front, where):
        rows = map_ref[:, where]
        row = rows[0:1]
        for k in range(1, rows.shape[0]):
            row = jnp.where(front == k, rows[k : k + 1], row)
        return row

    def row_pick(map_ref, front, blk, base, keep):
        pair = map_row(map_ref, front, pl.ds(pl.multiple_of(128 * (blk // 2), 128), 128))
        mine = jnp.where(lax.rem(blk, 2) == 0, pair[:, 0:64], pair[:, 64:128])
        want = base + lax.broadcasted_iota(jnp.int32, (64, 64), 0)
        return jnp.where((mine == want) & keep, 1.0, 0.0).astype(BF16)

    def picked(pick, block):
        hi, lo = split(block)
        both = dot16(pick, jnp.concatenate([hi, lo], 1)).astype(BF16)
        return jnp.concatenate([both[:, 0:256], both[:, 256:512]], 0)

    def expand(map_ref, fronts, picks, blocks, n, base):
        lhs = jnp.concatenate([picked(p, b) for p, b in zip(picks, blocks)], 1)
        maps = [map_row(map_ref, f, lanes(n)) for f in fronts]
        where_to = jnp.concatenate(maps, 1)
        out = []
        for start in (0, base):
            want = 256 * n + start + lax.broadcasted_iota(jnp.int32, (256, 512), 0)
            hot = jnp.where(where_to == want, 1.0, 0.0).astype(BF16)
            prod = dot16(lhs, hot, NT)
            out.append(prod[:64] + prod[64:])
        return out

    def g_rows(n):
        return g_ref[:, lanes(n)] - times_panel(wg_both, wg_hi, rows_of(pan_g, n))

    finish(gather_g)
    one_send[0] = g_rows(5)
    s_one = new_sem(1)
    send(one_send.at[0], one_recv.at[0], x_pair, s_one)
    g_slots = (0, 1, 2, 3, 4, 7)
    for i, n in enumerate(g_slots):
        ug_send[i] = g_rows(n)
    s_g = new_sem(1)
    send(ug_send, ug_recv, x_pair, s_g)
    blk_g = lax.rem(me, 32)
    keep_g = (blk_g < 24) | (blk_g >= 28)
    base_g = 64 * lax.rem(me, 64)
    fronts_g = (x, x + 1 - 2 * x2)
    picks_g = [row_pick(gm_ref, f, blk_g, base_g, keep_g) for f in fronts_g]

    def add_g(n, own, other):
        lo, hi = expand(gm_ref, fronts_g, picks_g, [own, other], n, 2048)
        c_acc[:, lanes(n)] += lo
        c_acc[:, lanes(n + 8)] += hi

    arrived(one_recv.at[0], s_one)
    add_g(5, one_send[0], one_recv[0])

    def c_rows(n):
        return c_acc[:, lanes(n)] - times_panel(wc_both, wc_hi, rows_of(pan_c, n))

    finish(gather_c)
    one_send[1] = c_rows(13)
    s_one = new_sem(1)
    send(one_send.at[1], one_recv.at[1], x_far, s_one)
    step(gather_1)
    blk_c = lax.rem(me, 64)
    keep_c = (blk_c < 56) | (blk_c >= 60)
    fronts_c = (x // 2, 1 - x // 2)
    picks_c = [row_pick(cm_ref, f, blk_c, 64 * me, keep_c) for f in fronts_c]

    arrived(one_recv.at[1], s_one)
    lo, hi = expand(cm_ref, fronts_c, picks_c, [one_send[1], one_recv[1]], 13, 4096)
    out_ref[:, 3328:3584] += lo
    own_0 = out_ref[:, 7424:7680] + hi
    pan_0[x, z, y, core] = own_0
    in_0 = (x == 3) & (z == 2) & (y >= 2)

    @pl.when(in_0)
    def _():
        dia_0[jnp.where(y == 3, 1, 0), core] = own_0

    spread_0 = spread_steps(dia_0, "root", 2, 2)
    gather_0 = gather_steps(pan_0, 4)
    step(spread_0, gather_0)

    def c_group(s):
        return jnp.where(s == 13, 15, s) if not isinstance(s, int) else s + 2 * (s == 13)

    def fill(s, _):
        uc_send[s] = c_rows(c_group(s))
        return 0

    s_c = new_sem(4)
    first, second = pl.ds(0, 7), pl.ds(7, 7)

    def relay():
        arrived(uc_relay.at[first], s_c)
        send(uc_relay.at[first], uc_recv.at[first], at(x + 1, z, y), s_c + 2)
        yield
        arrived(uc_relay.at[second], s_c + 1)
        send(uc_relay.at[second], uc_recv.at[second], at(x + 3, z, y), s_c + 3)
        yield
        arrived(uc_recv.at[first], s_c + 2)
        yield
        arrived(uc_recv.at[second], s_c + 3)
        yield

    def add_c(s):
        n = c_group(s)
        lo, hi = expand(cm_ref, fronts_c, picks_c, [uc_send[s], uc_recv[s]], n, 4096)
        out_ref[:, lanes(n)] += lo
        out_ref[:, lanes(n + 16)] += hi

    arrived(ug_recv, s_g)
    for i, n in enumerate(g_slots):
        add_g(n, ug_send[i], ug_recv[i])
        if i == 2:
            step(spread_0, gather_0)
    lax.fori_loop(0, 7, fill, 0)
    send(uc_send.at[first], uc_relay.at[first], at(x + 1, z, y), s_c)
    step(spread_0, gather_0, gather_1)
    lax.fori_loop(7, 14, fill, 0)
    send(uc_send.at[second], uc_relay.at[second], at(x + 3, z, y), s_c + 1)
    step(spread_0)
    step(gather_0)
    finish(spread_0)
    finish(gather_1)
    relay_c = relay()

    mat[0] = dia_0[...].reshape(256, 256)
    mat[1] = pan_1[3, 3, 0:2].reshape(256, 256)

    def root_block(k):
        def share():
            hi = 64 * k + 64
            cross = pan_1[3, 2, 2:4].reshape(256, 256)[0:hi]
            low = dot32(inv[0, 64 * k : hi, 0:hi], cross)
            low_x[64 * k : hi] = low
            mat[1] -= dot32(low, low, ((0,), (0,)))
        return [share]

    inverse_factor([mat.at[0]], [inv.at[0]], [tile.at[0]], timed({
        6: [gather_0], 18: [relay_c], 22: [relay_c], 30: [gather_0]}), root_block)

    def own_low():
        low = dot32(own_0, inv[0], NT)
        rf_ref[:, 0:256] = low

    def own_next():
        low = rf_ref[:, 0:256]
        own_1[...] = pan_1[x, z, y, core] - dot32(low, low_x[...])
        m_own[...] = dot32(low, inv[0])

    def cross_weight():
        x_mat[...] = dot32(low_x[...], inv[0], ((0,), (0,)))

    plan = {1: [own_low], 2: [own_next], 3: [cross_weight, relay_c], 14: [gather_0], 17: [relay_c]}
    for k in range(7):
        plan.setdefault(4 + 2 * k, []).append(lambda k=k: add_c(k))
        plan.setdefault(18 + 2 * k, []).append(lambda k=k: add_c(7 + k))
    inverse_factor([mat.at[1]], [inv.at[1]], [tile.at[1]], timed(plan))
    inv_1 = inv[1]

    low_1 = dot32(own_1[...], inv_1, NT)
    rf_ref[:, 256:512] = jnp.where(in_0, 0.0, low_1)
    w_1 = dot32(low_1, inv_1)
    m_0 = m_own[...] - dot32(w_1, x_mat[...])
    w_hi, w_lo = split(jnp.concatenate([m_0, w_1], 1))
    w_both = jnp.concatenate([w_hi, w_lo], 0)

    finish(relay_c)
    finish(gather_0)

    row_kept = jnp.logical_not((x == 3) & (((z == 2) & (y >= 2)) | ((z == 3) & (y < 2))))

    out_ref[:, 7424:7936] = jnp.zeros((64, 512), F32)

    def last(t, _):
        n = jnp.where(t >= 29, t + 2, t)
        panel = jnp.concatenate([rows_of(pan_0, n), rows_of(pan_1, n)], 1)
        res = out_ref[:, lanes(n)] - times_panel(w_both, w_hi, panel)
        out_ref[:, lanes(n)] = jnp.where(row_kept, res, 0.0)
        return 0

    for part in range(5):
        lax.fori_loop(6 * part, 6 * part + 6, last, 0)
        first_n, last_n = 6 * part, (6 * part + 6 if part < 4 else 32)
        where = slice(256 * first_n, 256 * last_n)
        pltpu.make_async_copy(out_ref.at[:, where], out_hbm.at[:, where], out_sems.at[part]).start()
    for part in range(5):
        first_n, last_n = 6 * part, (6 * part + 6 if part < 4 else 32)
        where = slice(256 * first_n, 256 * last_n)
        pltpu.make_async_copy(out_ref.at[:, where], out_hbm.at[:, where], out_sems.at[part]).wait()

    for copy, cond in pending:
        guarded(cond, copy.wait_send)


def local(gfront, cfront, rfront, gmap, cmap):
    vmem = pl.BlockSpec(memory_space=pltpu.VMEM)
    hbm = pl.BlockSpec(memory_space=pl.ANY)
    block = (64, 256)
    parts = pl.pallas_call(
        kernel,
        out_shape=(
            jax.ShapeDtypeStruct((64, 256), F32),
            jax.ShapeDtypeStruct((64, 256), F32),
            jax.ShapeDtypeStruct((64, 512), F32),
            jax.ShapeDtypeStruct((64, 8192), F32),
        ),
        in_specs=[hbm] * 5,
        out_specs=(vmem, vmem, vmem, hbm),
        scratch_shapes=[
            pltpu.VMEM((64, 2048), F32),
            pltpu.VMEM((64, 8192), F32),
            pltpu.VMEM((4, 2048), jnp.int32),
            pltpu.VMEM((2, 4096), jnp.int32),
            pltpu.VMEM((1, 4, 4, 2) + block, F32),
            pltpu.VMEM((2, 4, 4, 2) + block, F32),
            pltpu.VMEM((4, 4, 4, 2) + block, F32),
            pltpu.VMEM((4, 4, 4, 2) + block, F32),
            pltpu.VMEM((2, 2) + block, F32),
            pltpu.VMEM((2, 2) + block, F32),
            pltpu.VMEM((2, 2) + block, F32),
            pltpu.VMEM((2, 256, 256), F32),
            pltpu.VMEM((2, 256, 256), F32),
            pltpu.VMEM((2, 64, 128), F32),
            pltpu.VMEM((64, 4096), F32),
            pltpu.VMEM((6,) + block, F32),
            pltpu.VMEM((6,) + block, F32),
            pltpu.VMEM((14,) + block, F32),
            pltpu.VMEM((14,) + block, F32),
            pltpu.VMEM((14,) + block, F32),
            pltpu.VMEM((2,) + block, F32),
            pltpu.VMEM((2,) + block, F32),
            pltpu.VMEM((256, 256), F32),
            pltpu.VMEM((256, 256), F32),
            pltpu.VMEM((64, 256), F32),
            pltpu.VMEM((64, 256), F32),
            pltpu.SemaphoreType.DMA((MAX_COPIES,)),
            pltpu.SemaphoreType.DMA((MAX_COPIES,)),
            pltpu.SemaphoreType.DMA((10,)),
            pltpu.SemaphoreType.DMA((5,)),
        ],
        compiler_params=pltpu.CompilerParams(
            collective_id=0, has_side_effects=True, vmem_limit_bytes=60 * 1024 * 1024
        ),
    )(gfront, cfront, rfront, gmap, cmap)


    chunks = [(0, slice(0, 256)), (1, slice(0, 256)), (2, slice(0, 512))]
    chunks += [(3, slice(2048 * k, 2048 * k + 2048)) for k in range(4)]

    def write(*refs):
        src, dst, buf, sems = refs[:4], refs[4:8], refs[8:12], refs[12]
        reads = [pltpu.make_async_copy(src[a].at[:, w], buf[a].at[:, w], sems.at[0, k])
                 for k, (a, w) in enumerate(chunks)]
        writes = [pltpu.make_async_copy(buf[a].at[:, w], dst[a].at[:, w], sems.at[1, k])
                  for k, (a, w) in enumerate(chunks)]
        for copy in reads:
            copy.start()
        for read, write in zip(reads, writes):
            read.wait()
            write.start()
        for copy in writes:
            copy.wait()

    return pl.pallas_call(
        write,
        out_shape=[jax.ShapeDtypeStruct(p.shape, F32) for p in parts],
        in_specs=[hbm] * 4,
        out_specs=[hbm] * 4,
        scratch_shapes=[pltpu.VMEM(p.shape, F32) for p in parts] + [pltpu.SemaphoreType.DMA((2, len(chunks)))],
        compiler_params=pltpu.CompilerParams(vmem_limit_bytes=60 * 1024 * 1024),
    )(*parts)


def solution(mesh):
    rows = P("cube", None)
    return jax.shard_map(
        local,
        mesh=mesh,
        in_specs=(rows, rows, rows, P(), P()),
        out_specs=(rows, rows, rows, rows),
        check_vma=False,
    )
```
